32 devices in a mesh: layer: 2 (over core), feat: 4 (over z), width: 4 (over y, x).
Axes of the slice: x: 2, y: 2, z: 4, core: 2. Of those that a mesh axis runs over, the one named last changes fastest.
Arguments:
- residual: bfloat16 [2, 1024, 8192], P('layer', None, 'width'), may hold values from -6 to 6
- encoder: bfloat16 [2, 8192, 16384], P('layer', 'width', 'feat'), may hold values from -0.0625 to 0.0625
- thresholds: float32 [2, 16384], P('layer', 'feat'), may hold values from 0.2 to 1
- active: int32 [2, 48], replicated, may hold values from 0 to 127, as said below
- self_decoder: bfloat16 [2, 16384, 8192], P('layer', 'feat', 'width'), may hold values from -0.15625 to 0.15625
- cross_decoder: bfloat16 [16384, 8192], P('feat', 'width'), may hold values from -0.15625 to 0.15625
Outputs:
- recon: bfloat16 [2, 1024, 8192], P('layer', 'feat', 'width')
The draws below stay inside these ranges and needn't reach their ends.
Inputs may be any that keep to these rules, and one draw needn't show every extreme that they name: `active`: each row lists 48 distinct block numbers.
All inputs are finite; a program needn't handle non-finite values.
Results may differ from the reference program's by a relative error of at most 0.0049.
Values may be sent and summed in bfloat16 or wider, within the bound.
No kernel may reach another device: no remote copies, remote signals or barrier semaphores. Data moves between devices by JAX's collectives and lax.ppermute only.
A program may use at most 128 MiB of HBM per device.

```python
import jax
import jax.numpy as jnp

D = 8192
BLOCKS = 128
BLOCK = 128
ACTIVE = 48
LAYERS = 2
TOK = 1024
F = 16384


def draw_active(key, part):
    keys_all = jax.random.split(jax.random.fold_in(key, 17), LAYERS)
    picked = jax.vmap(lambda single: jax.random.permutation(single, BLOCKS)[:ACTIVE])(keys_all)
    return picked.astype(jnp.int32)


def steps_of(rng, dims, cuts, smallest, high):
    def one(position, shards_of):
        draws = jax.random.uniform(jax.random.fold_in(jax.random.fold_in(rng, 6), position), (shards_of,), jnp.float32, smallest / len(cuts), high / len(cuts))
        return jnp.repeat(jnp.exp(draws), dims[position] // shards_of).reshape((-1,) + (1,) * (len(dims) - position - 1))

    loudness = one(*cuts[0])
    for cut in cuts[1:]:
        loudness = loudness * one(*cut)
    return loudness


def scatter_about(own_key, shape, deviation, reach, cuts=(), held_as=jnp.bfloat16):
    level = steps_of(own_key, shape, cuts, -0.22, 0.18) if cuts else 1.0
    drawn = jax.random.normal(own_key, shape, jnp.float32) * deviation * level
    return jnp.minimum(jnp.maximum(drawn, -reach), reach).astype(held_as)


def setup_inputs(seed: int = 0) -> dict:
    arg_keys = jax.random.split(jax.random.key(seed), 7)
    return {
        "residual": scatter_about(arg_keys[0], (LAYERS, TOK, D), 1.0, 6.0, ((0, 2), (2, 4))),
        "encoder": scatter_about(arg_keys[1], (LAYERS, D, F), D ** -0.5, 0.0625, ((0, 2), (1, 4), (2, 4))),
        "thresholds": jnp.clip(0.2 + 0.8 * jax.random.uniform(arg_keys[2], (LAYERS, F), jnp.float32) ** steps_of(arg_keys[2], (LAYERS, F), ((0, 2), (1, 4)), -0.2, 0.2), 0.2, 1.0),
        "active": draw_active(jax.random.fold_in(arg_keys[6], 71), 0),
        "self_decoder": scatter_about(arg_keys[4], (LAYERS, F, D), (ACTIVE * BLOCK // 4) ** -0.5, 0.15625, ((0, 2), (1, 4), (2, 4))),
        "cross_decoder": scatter_about(arg_keys[5], (F, D), (ACTIVE * BLOCK // 4) ** -0.5, 0.15625, ((0, 4), (1, 4))),
    }


def block_keep(chosen):
    ident = jnp.arange(F, dtype=jnp.int32) // BLOCK
    return jnp.any(chosen[:, None] == ident[None, :], axis=0).astype(jnp.float32)


def reference(residual, encoder, thresholds, active, self_decoder, cross_decoder):
    codes_all = []
    for source in range(LAYERS):
        pre = jnp.dot(residual[source], encoder[source], preferred_element_type=jnp.float32)
        keep = block_keep(active[source])
        codes_all.append((jnp.maximum(pre - thresholds[source][None, :], 0.0) * keep[None, :]).astype(jnp.bfloat16))
    first = jnp.dot(codes_all[0], self_decoder[0], preferred_element_type=jnp.float32)
    second = jnp.dot(codes_all[1], self_decoder[1], preferred_element_type=jnp.float32)
    second = second + jnp.dot(codes_all[0], cross_decoder, preferred_element_type=jnp.float32)
    return jnp.stack([first.astype(jnp.bfloat16), second.astype(jnp.bfloat16)], axis=0)
```

```python
import functools

import jax
import jax.numpy as jnp
import numpy as np
from jax import lax
from jax.experimental import pallas as pl
from jax.experimental.pallas import tpu as pltpu
from jax.sharding import PartitionSpec as P

BLOCK = 128
MIB = 1 << 20


def capacities(blocks, listed, shards):
    most = min(blocks, listed)
    top = min(blocks, -(-most // 4) * 4)
    fair = -(-listed // shards)
    first = -(-(fair * 4) // 12) * 4
    return sorted({c for c in (first, first + 4) if c < top} | {top})


def target_order(count):
    rows = []
    for i in range(count):
        rows.append(sorted(range(count), key=lambda t: (-abs(t - i), t < i)))
    return rows


def encode_kernel(parts, rows_ref, ids_ref, *refs):
    del rows_ref, ids_ref
    pieces = refs[: parts[0] * parts[1]]
    left, right = refs[len(pieces) : len(pieces) + 2]
    outs = refs[len(pieces) + 2 : -1]
    lhs = refs[-1]
    unit = pieces[0].shape[0]

    @pl.when(pl.program_id(0) == 0)
    def _():
        for k, piece in enumerate(pieces):
            lhs[k * unit : (k + 1) * unit, :] = piece[...]

    weight = jnp.concatenate([left[...], right[...]], axis=1)
    total = jnp.dot(lhs[...], weight, preferred_element_type=jnp.float32)
    size = unit * parts[1]
    for p, out in enumerate(outs):
        out[...] = total[p * size : (p + 1) * size, :].astype(out.dtype)


def encode(residual, encoder, rows, ids, width, units, unit):
    depth = residual.shape[1]
    slots = ids.shape[0]
    feats = slots * BLOCK
    count = width * units
    size = units * unit
    in_specs = [
        pl.BlockSpec((unit, depth), functools.partial(lambda k, j, r, i: (r[k], 0), k))
        for k in range(count)
    ] + [
        pl.BlockSpec(
            (None, depth, BLOCK), functools.partial(lambda q, j, r, i: (0, 0, i[2 * j + q]), q)
        )
        for q in range(2)
    ]
    out_specs = [pl.BlockSpec((size, 2 * BLOCK), lambda j, r, i: (0, j)) for _ in range(width)]
    out_shape = [
        jax.ShapeDtypeStruct((size, feats), jnp.float32 if p == 0 else jnp.bfloat16)
        for p in range(width)
    ]
    return pl.pallas_call(
        functools.partial(encode_kernel, (width, units)),
        out_shape=out_shape,
        grid_spec=pltpu.PrefetchScalarGridSpec(
            num_scalar_prefetch=2,
            grid=(slots // 2,),
            in_specs=in_specs,
            out_specs=out_specs,
            scratch_shapes=[pltpu.VMEM((count * unit, depth), jnp.bfloat16)],
        ),
        compiler_params=pltpu.CompilerParams(vmem_limit_bytes=16 * MIB),
        cost_estimate=pl.CostEstimate(
            flops=2 * count * unit * depth * feats,
            bytes_accessed=2 * depth * feats,
            transcendentals=0,
        ),
        name="encode",
    )(rows, ids, *([residual] * count), encoder, encoder)


def decode_kernel(flag_ref, own_ids, source_ids, own, source, *refs):
    del own_ids, source_ids
    own_w, source_w, out = refs[:4], refs[4:8], refs[8]
    phase, j = pl.program_id(0), pl.program_id(1)

    @pl.when((phase == 0) & (j == 0))
    def _():
        out[...] = jnp.zeros_like(out)

    @pl.when(phase == 0)
    def _():
        weight = jnp.concatenate([w[...] for w in own_w], axis=0)
        out[...] += jnp.dot(own[...], weight, preferred_element_type=jnp.float32)

    @pl.when((phase == 1) & (flag_ref[0] == 1))
    def _():
        weight = jnp.concatenate([w[...] for w in source_w], axis=0)
        out[...] += jnp.dot(source[...], weight, preferred_element_type=jnp.float32)


def decode(codes, source, self_decoder, cross_decoder, flag, own_ids, source_ids):
    tokens, feats = codes.shape
    width = cross_decoder.shape[1]
    slots = own_ids.shape[0]
    steps = slots // 4

    def own_at(phase, j):
        return jnp.where(phase == 0, j, steps - 1)

    def source_at(phase, j, flag_ref):
        return jnp.where((phase == 1) & (flag_ref[0] == 1), j, 0)

    in_specs = [
        pl.BlockSpec((tokens, 4 * BLOCK), lambda p, j, f, a, b: (0, own_at(p, j))),
        pl.BlockSpec((tokens, 4 * BLOCK), lambda p, j, f, a, b: (0, source_at(p, j, f))),
    ]
    for q in range(4):
        in_specs.append(
            pl.BlockSpec(
                (None, BLOCK, width),
                functools.partial(lambda q, p, j, f, a, b: (0, a[4 * own_at(p, j) + q], 0), q),
            )
        )
    for q in range(4):
        in_specs.append(
            pl.BlockSpec(
                (BLOCK, width),
                functools.partial(lambda q, p, j, f, a, b: (b[4 * source_at(p, j, f) + q], 0), q),
            )
        )
    return pl.pallas_call(
        decode_kernel,
        out_shape=jax.ShapeDtypeStruct((tokens, width), jnp.float32),
        grid_spec=pltpu.PrefetchScalarGridSpec(
            num_scalar_prefetch=3,
            grid=(2, steps),
            in_specs=in_specs,
            out_specs=pl.BlockSpec((tokens, width), lambda p, j, f, a, b: (0, 0)),
        ),
        compiler_params=pltpu.CompilerParams(vmem_limit_bytes=24 * MIB),
        cost_estimate=pl.CostEstimate(
            flops=4 * tokens * width * feats,
            bytes_accessed=4 * width * feats,
            transcendentals=0,
        ),
        name="decode",
    )(flag, own_ids, source_ids, codes, source, *([self_decoder] * 4), *([cross_decoder] * 4))


def finish_kernel(place_ref, own, first, second, out):
    del place_ref
    total = own[...] + first[...].astype(jnp.float32) + second[...].astype(jnp.float32)
    out[...] = total.astype(out.dtype)


def finish(place, own, first, second):
    count = place.shape[0]
    tokens, width = own.shape
    spec = pl.BlockSpec((tokens // count, width), lambda p, r: (p, 0))
    return pl.pallas_call(
        finish_kernel,
        out_shape=jax.ShapeDtypeStruct((tokens, width), jnp.bfloat16),
        grid_spec=pltpu.PrefetchScalarGridSpec(
            num_scalar_prefetch=1,
            grid=(count,),
            in_specs=[spec] * 3,
            out_specs=pl.BlockSpec((tokens // count, width), lambda p, r: (r[p], 0)),
        ),
        compiler_params=pltpu.CompilerParams(vmem_limit_bytes=8 * MIB),
        name="finish",
    )(place, own, first, second)


def slot_ids(present, slots):
    count = jnp.sum(present.astype(jnp.int32))
    rank = jnp.cumsum(present.astype(jnp.int32)) - 1
    slot = jnp.minimum(jnp.arange(slots, dtype=jnp.int32), jnp.maximum(count - 1, 0))
    hit = present[None, :] & (rank[None, :] == slot[:, None])
    block = jnp.arange(present.shape[0], dtype=jnp.int32)
    return jnp.sum(jnp.where(hit, block[None, :], 0), axis=1), count


def run(slots, residual, encoder, thresholds, own_present, source_present, self_decoder, cross_decoder):
    layer_index = lax.axis_index("layer")
    feat_index = lax.axis_index("feat")
    width_index = lax.axis_index("width")
    feat_count = lax.axis_size("feat")
    width_count = lax.axis_size("width")
    tokens = residual.shape[0]
    chunks = min(4, feat_count)
    units = feat_count // chunks
    block = tokens // feat_count
    unit = block // width_count
    size = units * unit
    feats = slots * BLOCK

    own_ids, own_count = slot_ids(own_present, slots)
    source_ids, _ = slot_ids(source_present, slots)
    kept = (jnp.arange(slots, dtype=jnp.int32) < own_count).astype(jnp.float32)
    keep = jnp.repeat(kept, BLOCK)[None, :]
    limit = jnp.take(thresholds.reshape(-1, BLOCK), own_ids, axis=0).reshape(1, feats)
    flag = (layer_index == 1).astype(jnp.int32).reshape(1)
    order = target_order(feat_count)
    mine = jnp.asarray(np.array(order, np.int32))[feat_index]
    place = width_index ^ jnp.arange(width_count, dtype=jnp.int32)

    def swap(value, p):
        return lax.ppermute(value, "width", [(w, w ^ p) for w in range(width_count)])

    decoded = []
    for c in range(chunks):
        wanted = lax.slice_in_dim(mine, c * units, (c + 1) * units)
        rows = (wanted[None, :] * width_count + place[:, None]).reshape(-1)
        own, *others = encode(residual, encoder, rows, own_ids, width_count, units, unit)
        arrived = [swap(other, p + 1) for p, other in enumerate(others)]
        total = own
        for term in arrived:
            total = total + term.astype(jnp.float32)
        share = (jnp.maximum(total - limit, 0.0) * keep).astype(jnp.bfloat16)
        pieces = [share] + [swap(share, p) for p in range(1, width_count)]
        codes = jnp.concatenate(pieces, axis=0)
        source = lax.ppermute(codes, "layer", [(0, 1)])
        result = decode(codes, source, self_decoder, cross_decoder, flag, own_ids, source_ids)
        split = result.reshape(width_count, units, unit, -1)
        for u in range(units):
            decoded.append(split[:, u].reshape(block, -1))

    def chosen(positions):
        groups = {}
        for device, position in positions.items():
            groups.setdefault(position, []).append(device)
        items = sorted(groups.items(), key=lambda item: -len(item[1]))
        value = decoded[items[0][0]]
        for position, devices in items[1:]:
            here = functools.reduce(jnp.logical_or, [feat_index == d for d in devices])
            value = jnp.where(here, decoded[position], value)
        return value

    zero = jnp.zeros((block, self_decoder.shape[2]), jnp.bfloat16)
    from_left, from_right = zero, zero
    for step in range(1, feat_count):
        up = {i: order[i].index(feat_count - step + i) for i in range(step)}
        down = {
            i: order[i].index(step - feat_count + i)
            for i in range(feat_count - step, feat_count)
        }
        upward, downward = chosen(up), chosen(down)
        if step > 1:
            upward = upward + from_left.astype(jnp.float32)
            downward = downward + from_right.astype(jnp.float32)
        from_left = lax.ppermute(
            upward.astype(jnp.bfloat16), "feat", [(i, i + 1) for i in sorted(up)]
        )
        from_right = lax.ppermute(
            downward.astype(jnp.bfloat16), "feat", [(i, i - 1) for i in sorted(down)]
        )
    return finish(place, decoded[-1], from_left, from_right)


def on_device(residual, encoder, thresholds, active, self_decoder, cross_decoder):
    layer_index = lax.axis_index("layer")
    feat_index = lax.axis_index("feat")
    feat_count = lax.axis_size("feat")
    blocks = encoder.shape[2] // BLOCK
    ident = jnp.arange(feat_count * blocks, dtype=jnp.int32)
    listed = jnp.any(active[:, :, None] == ident[None, None, :], axis=1)
    listed = listed.reshape(active.shape[0], feat_count, blocks)
    most = jnp.max(jnp.sum(listed.astype(jnp.int32), axis=2))
    here = lax.dynamic_index_in_dim(listed, feat_index, 1, keepdims=False)
    own_present = lax.dynamic_index_in_dim(here, layer_index, 0, keepdims=False)
    source_present = here[0]
    sizes = capacities(blocks, active.shape[1], feat_count)
    branch = sum((most > s).astype(jnp.int32) for s in sizes[:-1]) if len(sizes) > 1 else 0
    out = lax.switch(
        branch,
        [functools.partial(run, s) for s in sizes],
        residual[0],
        encoder,
        thresholds[0],
        own_present,
        source_present,
        self_decoder,
        cross_decoder,
    )
    return out[None]


def solution(mesh):
    in_specs = (
        P("layer", None, "width"),
        P("layer", "width", "feat"),
        P("layer", "feat"),
        P(),
        P("layer", "feat", "width"),
        P("feat", "width"),
    )
    out_specs = P("layer", "feat", "width")
    return jax.shard_map(
        on_device, mesh=mesh, in_specs=in_specs, out_specs=out_specs, check_vma=False
    )
```

```python
import functools

import jax
import jax.numpy as jnp
import numpy as np
from jax import lax
from jax.experimental import pallas as pl
from jax.experimental.pallas import tpu as pltpu
from jax.sharding import PartitionSpec as P


BLOCK = 128
MIB = 1 << 20
GRANT = [8 * MIB]
TILE = 4 * BLOCK


def capacities(blocks, listed, shards):
    most = min(blocks, listed)
    fair = -(-listed // shards)
    first = -(-(fair * 4) // 12) * 4
    if most <= first:
        return [(1, -(-most // 2) * 2)]
    once = [(1, first)] + ([(1, first + 4)] if first + 4 < most else [])
    return once + [(-(-most // first), first)]


def target_order(count):
    rows = []
    for i in range(count):
        rows.append(sorted(range(count), key=lambda t: (-abs(t - i), t < i)))
    return rows


def slots_of(active_ref, layer, first, blocks, start, ids):
    slots = ids.shape[0]
    for k in range(slots):
        ids[k] = 0

    def look(k, count):
        block = active_ref[layer, k] - first
        here = (block >= 0) & (block < blocks)

        @pl.when(here & (count >= 0) & (count < slots))
        def _():
            ids[count] = block

        return count + here.astype(jnp.int32)

    return lax.fori_loop(0, active_ref.shape[1], look, -start, unroll=8)


def load_kernel(shape, active, place, order, residual, encoder, thresholds, weight, tokens, limit, *refs):
    blocks, width, units, unit = shape
    outs, (ids, sems, more) = refs[:width], refs[width:]
    slots = ids.shape[0]
    tile = 2 * BLOCK
    size = units * unit

    def row_copy(k):
        chunk, p, u = k // (width * units), k // units % width, k % units
        row = order[place[1], chunk * units + u] * width + (place[2] ^ p)
        return pltpu.make_async_copy(
            residual.at[pl.ds(pl.multiple_of(row * unit, unit), unit), :],
            tokens.at[k * unit : (k + 1) * unit, :],
            more.at[k],
        )

    def block_copy(k, block):
        return pltpu.make_async_copy(
            encoder.at[0, :, pl.ds(pl.multiple_of(block * BLOCK, BLOCK), BLOCK)],
            weight.at[:, pl.ds(pl.multiple_of(k * BLOCK, BLOCK), BLOCK)],
            sems.at[k],
        )

    copies = [row_copy(k) for k in range(tokens.shape[0] // unit)]
    early = width * units
    for copy in copies[:early]:
        copy.start()
    count = slots_of(active, place[0], place[1] * blocks, blocks, place[3], ids)
    for k in range(slots):
        block_copy(k, ids[k]).start()
    for copy in copies[early:]:
        copy.start()
    for k in range(slots):
        row = thresholds[pl.ds(ids[k], 1), :]
        limit[:, k * BLOCK : (k + 1) * BLOCK] = jnp.where(k < count, row, jnp.inf)
    for copy in copies[:early]:
        copy.wait()

    @pl.loop(0, slots // 2)
    def _(n):
        block_copy(2 * n, 0).wait()
        block_copy(2 * n + 1, 0).wait()
        at = pl.ds(pl.multiple_of(n * tile, tile), tile)
        total = jnp.dot(
            tokens[: width * size, :], weight[:, at], preferred_element_type=jnp.float32
        )
        for p, out in enumerate(outs):
            out[:, at] = total[p * size : (p + 1) * size, :].astype(out.dtype)

    for copy in copies[early:]:
        copy.wait()


def load(active, place, order, residual, encoder, thresholds, slots, width, units, unit):
    depth = residual.shape[1]
    feats = slots * BLOCK
    blocks = encoder.shape[2] // BLOCK
    smem = pl.BlockSpec(memory_space=pltpu.SMEM)
    anywhere = pl.BlockSpec(memory_space=pl.ANY)
    vmem = pl.BlockSpec(memory_space=pltpu.VMEM)
    return pl.pallas_call(
        functools.partial(load_kernel, (blocks, width, units, unit)),
        out_shape=[
            jax.ShapeDtypeStruct((depth, feats), jnp.bfloat16),
            jax.ShapeDtypeStruct(residual.shape, jnp.bfloat16),
            jax.ShapeDtypeStruct((1, feats), jnp.float32),
        ]
        + [
            jax.ShapeDtypeStruct((units * unit, feats), jnp.float32 if p == 0 else jnp.bfloat16)
            for p in range(width)
        ],
        in_specs=[smem, smem, smem, anywhere, anywhere, vmem],
        out_specs=[vmem] * (3 + width),
        scratch_shapes=[
            pltpu.SMEM((slots,), jnp.int32),
            pltpu.SemaphoreType.DMA((slots,)),
            pltpu.SemaphoreType.DMA((residual.shape[0] // unit,)),
        ],
        compiler_params=pltpu.CompilerParams(vmem_limit_bytes=GRANT[-1]),
        cost_estimate=pl.CostEstimate(
            flops=0, bytes_accessed=2 * depth * (feats + residual.shape[0]), transcendentals=0
        ),
        name="load",
    )(active, place, order, residual, encoder, thresholds)


def fetch_kernel(blocks, active, place, after, own_w, source_w, own_out, source_out, own_ids, source_ids, sems):
    del after
    first = place[1] * blocks
    slots = own_ids.shape[0]
    slots_of(active, place[0], first, blocks, place[3], own_ids)
    slots_of(active, 0, first, blocks, place[3], source_ids)
    copies = []
    for k in range(slots):
        there = slice(k * BLOCK, (k + 1) * BLOCK)
        source = own_w.at[0, pl.ds(pl.multiple_of(own_ids[k] * BLOCK, BLOCK), BLOCK), :]
        copies.append(pltpu.make_async_copy(source, own_out.at[there, :], sems.at[0, k]))
        source = source_w.at[pl.ds(pl.multiple_of(source_ids[k] * BLOCK, BLOCK), BLOCK), :]
        copies.append(pltpu.make_async_copy(source, source_out.at[there, :], sems.at[1, k]))
    for copy in copies:
        copy.start()
    for copy in copies:
        copy.wait()


def fetch(active, place, after, self_decoder, cross_decoder, slots):
    width = cross_decoder.shape[1]
    blocks = cross_decoder.shape[0] // BLOCK
    smem = pl.BlockSpec(memory_space=pltpu.SMEM)
    anywhere = pl.BlockSpec(memory_space=pl.ANY)
    vmem = pl.BlockSpec(memory_space=pltpu.VMEM)
    return pl.pallas_call(
        functools.partial(fetch_kernel, blocks),
        out_shape=[jax.ShapeDtypeStruct((slots * BLOCK, width), jnp.bfloat16)] * 2,
        in_specs=[smem, smem, anywhere, anywhere, anywhere],
        out_specs=[vmem, vmem],
        scratch_shapes=[
            pltpu.SMEM((slots,), jnp.int32),
            pltpu.SMEM((slots,), jnp.int32),
            pltpu.SemaphoreType.DMA((2, slots)),
        ],
        compiler_params=pltpu.CompilerParams(vmem_limit_bytes=GRANT[-1]),
        cost_estimate=pl.CostEstimate(
            flops=0, bytes_accessed=4 * slots * BLOCK * width, transcendentals=0
        ),
        name="fetch",
    )(active, place, after, self_decoder, cross_decoder)


def encode_kernel(first, after, tokens, weight, *outs):
    del after
    size = outs[0].shape[0]
    count = size * len(outs)
    tile = 2 * BLOCK
    lhs = tokens[first : first + count, :]

    @pl.loop(0, weight.shape[1] // tile)
    def _(n):
        at = pl.ds(pl.multiple_of(n * tile, tile), tile)
        total = jnp.dot(lhs, weight[:, at], preferred_element_type=jnp.float32)
        for p, out in enumerate(outs):
            out[:, at] = total[p * size : (p + 1) * size, :].astype(out.dtype)


def encode(tokens, weight, chunk, chunks, width, after):
    size = tokens.shape[0] // (chunks * width)
    depth, feats = weight.shape
    vmem = pl.BlockSpec(memory_space=pltpu.VMEM)
    return pl.pallas_call(
        functools.partial(encode_kernel, chunk * width * size),
        out_shape=[
            jax.ShapeDtypeStruct((size, feats), jnp.float32 if p == 0 else jnp.bfloat16)
            for p in range(width)
        ],
        in_specs=[pl.BlockSpec(memory_space=pl.ANY), vmem, vmem],
        out_specs=[vmem] * width,
        compiler_params=pltpu.CompilerParams(vmem_limit_bytes=GRANT[-1]),
        cost_estimate=pl.CostEstimate(
            flops=2 * width * size * depth * feats, bytes_accessed=0, transcendentals=0
        ),
        name="encode",
    )(after, tokens, weight)


def combine_kernel(own, limit, *refs):
    out = refs[-1]
    tile = 2 * BLOCK

    @pl.loop(0, out.shape[1] // tile)
    def _(n):
        at = pl.ds(pl.multiple_of(n * tile, tile), tile)
        total = own[:, at]
        for term in refs[:-1]:
            total = total + term[:, at].astype(jnp.float32)
        out[:, at] = jnp.maximum(total - limit[:, at], 0.0).astype(out.dtype)


def combine(own, limit, arrived):
    vmem = pl.BlockSpec(memory_space=pltpu.VMEM)
    return pl.pallas_call(
        combine_kernel,
        out_shape=jax.ShapeDtypeStruct(own.shape, jnp.bfloat16),
        in_specs=[vmem] * (2 + len(arrived)),
        out_specs=vmem,
        compiler_params=pltpu.CompilerParams(vmem_limit_bytes=GRANT[-1]),
        cost_estimate=pl.CostEstimate(flops=0, bytes_accessed=own.size * 4, transcendentals=0),
        name="combine",
    )(own, limit, *arrived)


def pack_kernel(*refs):
    out = refs[-1]
    size = refs[0].shape[0]
    for p, piece in enumerate(refs[:-1]):
        out[p * size : (p + 1) * size, :] = piece[...]


def pack(pieces):
    vmem = pl.BlockSpec(memory_space=pltpu.VMEM)
    size, feats = pieces[0].shape
    return pl.pallas_call(
        pack_kernel,
        out_shape=jax.ShapeDtypeStruct((size * len(pieces), feats), jnp.bfloat16),
        in_specs=[vmem] * len(pieces),
        out_specs=vmem,
        compiler_params=pltpu.CompilerParams(vmem_limit_bytes=GRANT[-1]),
        cost_estimate=pl.CostEstimate(flops=0, bytes_accessed=0, transcendentals=0),
        name="pack",
    )(*pieces)


def decode_kernel(codes, weight, out):
    @pl.loop(0, out.shape[1] // TILE)
    def _(n):
        at = pl.ds(pl.multiple_of(n * TILE, TILE), TILE)
        out[:, at] = jnp.dot(codes[...], weight[:, at], preferred_element_type=jnp.float32)


def decode_more_kernel(codes, weight, base, out, *rounded):
    @pl.loop(0, out.shape[1] // TILE)
    def _(n):
        at = pl.ds(pl.multiple_of(n * TILE, TILE), TILE)
        total = base[:, at] + jnp.dot(
            codes[...], weight[:, at], preferred_element_type=jnp.float32
        )
        out[:, at] = total
        for ref in rounded:
            ref[:, at] = total.astype(ref.dtype)


def decode(codes, weight, base=None, both=True):
    vmem = pl.BlockSpec(memory_space=pltpu.VMEM)
    tokens, feats = codes.shape
    width = weight.shape[1]
    extra = () if base is None else (base,)
    out_shape = [jax.ShapeDtypeStruct((tokens, width), jnp.float32)]
    if base is not None and both:
        out_shape.append(jax.ShapeDtypeStruct((tokens, width), jnp.bfloat16))
    return pl.pallas_call(
        decode_kernel if base is None else decode_more_kernel,
        out_shape=out_shape,
        in_specs=[vmem] * (2 + len(extra)),
        out_specs=[vmem] * len(out_shape),
        compiler_params=pltpu.CompilerParams(vmem_limit_bytes=GRANT[-1]),
        cost_estimate=pl.CostEstimate(
            flops=2 * tokens * feats * width, bytes_accessed=0, transcendentals=0
        ),
        name="decode" if base is None else "decode_more",
    )(codes, weight, *extra)


def relay_kernel(owners, place, came, *refs):
    out = refs[-1]
    for devices, value in zip(owners, refs[:-1], strict=True):
        here = functools.reduce(jnp.logical_or, [place[1] == d for d in devices])

        @pl.when(here)
        def _(value=value):
            out[...] = (value[...] + came[...].astype(jnp.float32)).astype(out.dtype)


def relay(owners, place, came, values):
    vmem = pl.BlockSpec(memory_space=pltpu.VMEM)
    return pl.pallas_call(
        functools.partial(relay_kernel, owners),
        out_shape=jax.ShapeDtypeStruct(came.shape, jnp.bfloat16),
        in_specs=[pl.BlockSpec(memory_space=pltpu.SMEM)] + [vmem] * (1 + len(values)),
        out_specs=vmem,
        compiler_params=pltpu.CompilerParams(vmem_limit_bytes=GRANT[-1]),
        cost_estimate=pl.CostEstimate(flops=0, bytes_accessed=4 * came.size, transcendentals=0),
        name="relay",
    )(place, came, *values)


def finish_kernel(place_ref, own, first, second, out):
    del place_ref
    total = own[...] + first[...].astype(jnp.float32) + second[...].astype(jnp.float32)
    out[...] = total.astype(out.dtype)


def finish(place, own, first, second, count):
    tokens, width = own.shape
    spec = pl.BlockSpec((tokens // count, width), lambda p, r: (p, 0))
    return pl.pallas_call(
        finish_kernel,
        out_shape=jax.ShapeDtypeStruct((tokens, width), jnp.bfloat16),
        grid_spec=pltpu.PrefetchScalarGridSpec(
            num_scalar_prefetch=1,
            grid=(count,),
            in_specs=[spec] * 3,
            out_specs=pl.BlockSpec((tokens // count, width), lambda p, r: (r[2] ^ p, 0)),
        ),
        compiler_params=pltpu.CompilerParams(vmem_limit_bytes=8 * MIB),
        name="finish",
    )(place, own, first, second)


def run(passes, slots, residual, encoder, thresholds, active, self_decoder, cross_decoder):
    layer_index = lax.axis_index("layer")
    feat_index = lax.axis_index("feat")
    width_index = lax.axis_index("width")
    feat_count = lax.axis_size("feat")
    width_count = lax.axis_size("width")
    tokens = residual.shape[0]
    chunks = min(4, feat_count)
    units = feat_count // chunks
    block = tokens // feat_count
    unit = block // width_count

    order = target_order(feat_count)
    table = jnp.asarray(np.array(order, np.int32))

    def setup(start):
        spot = [jnp.asarray(n, jnp.int32) for n in (layer_index, feat_index, width_index, start)]
        place = jnp.stack(spot)
        loaded = load(
            active, place, table, residual, encoder, thresholds, slots, width_count, units, unit
        )
        weights = fetch(active, place, loaded[4], self_decoder, cross_decoder, slots)
        return place, loaded, weights

    def swap(value, p):
        return lax.ppermute(value, "width", [(w, w ^ p) for w in range(width_count)])

    def spread(values):
        moved = []
        for p, value in enumerate(values, 1):
            moved.append(swap(value, p))
        return moved

    def chunk_of(limit, own, others, weights, base=None):
        own_w, source_w = weights
        arrived = spread(others)
        share = combine(own, limit, arrived)
        pieces = [share] + spread([share] * (width_count - 1))
        codes = pack(pieces)
        source = lax.ppermute(codes, "layer", [(0, 1)])
        (base,) = decode(codes, own_w, base, False)
        return decode(source, source_w, base)

    results = []
    if passes > 1:
        part = tokens // chunks

        def one_pass(g, kept):
            place, (weight, ordered, limit, *_), weights = setup(g * slots)

            def one(c, kept):
                some = lax.dynamic_slice_in_dim(ordered, c * part, part)
                own, *others = encode(some, weight, 0, 1, width_count, limit)
                before = lax.dynamic_slice_in_dim(kept, c * part, part)
                result, _ = chunk_of(limit, own, others, weights, before)
                return lax.dynamic_update_slice_in_dim(kept, result, c * part, 0)

            return lax.fori_loop(0, chunks, one, kept)

        kept = jnp.zeros((tokens, cross_decoder.shape[1]), jnp.float32)
        kept = lax.fori_loop(0, passes, one_pass, kept)
        place = jnp.stack([layer_index, feat_index, width_index]).astype(jnp.int32)
        results = [(result, result.astype(jnp.bfloat16)) for result in jnp.split(kept, chunks)]
    else:
        place, (weight, ordered, limit, own, *others), weights = setup(0)
        for c in range(chunks):
            if c > 0:
                own, *others = encode(ordered, weight, c, chunks, width_count, limit)
            results.append(chunk_of(limit, own, others, weights))
    decoded = []
    for result, rounded in results:
        wide = result.reshape(width_count, units, unit, -1)
        thin = rounded.reshape(width_count, units, unit, -1)
        for u in range(units):
            if units == 1:
                decoded.append((result, rounded))
            else:
                decoded.append((wide[:, u].reshape(block, -1), thin[:, u].reshape(block, -1)))

    def next_sum(positions, came):
        owners = {}
        for device, position in positions.items():
            owners.setdefault(position, []).append(device)
        used = sorted(owners)
        if came is None:
            return decoded[used[0]][1]
        devices = tuple(tuple(owners[k]) for k in used)
        return relay(devices, place, came, [decoded[k][0] for k in used])

    from_left = from_right = None
    for step in range(1, feat_count):
        up = {i: order[i].index(feat_count - step + i) for i in range(step)}
        down = {
            i: order[i].index(step - feat_count + i)
            for i in range(feat_count - step, feat_count)
        }
        upward = next_sum(up, from_left)
        downward = next_sum(down, from_right)
        from_left = lax.ppermute(upward, "feat", [(i, i + 1) for i in sorted(up)])
        from_right = lax.ppermute(downward, "feat", [(i, i - 1) for i in sorted(down)])
    return finish(place, decoded[-1][0], from_left, from_right, width_count)


def layered(passes, slots, *args):
    if passes == 1:
        return run(passes, slots, *args)
    GRANT.append(40 * MIB)
    try:
        return run(passes, slots, *args)
    finally:
        GRANT.pop()


def on_device(residual, encoder, thresholds, active, self_decoder, cross_decoder):
    feat_count = lax.axis_size("feat")
    blocks = encoder.shape[2] // BLOCK
    low = blocks * jnp.arange(feat_count, dtype=jnp.int32)[None, :, None]
    inside = (active[:, None, :] >= low) & (active[:, None, :] < low + blocks)
    counts = jnp.sum(inside.astype(jnp.int32), axis=2)
    most = jnp.max(counts)
    sizes = capacities(blocks, active.shape[1], feat_count)
    branch = sum((most > s).astype(jnp.int32) for _, s in sizes[:-1]) if len(sizes) > 1 else 0
    out = lax.switch(
        branch,
        [functools.partial(layered, *size) for size in sizes],
        residual[0],
        encoder,
        thresholds[0].reshape(-1, BLOCK),
        active,
        self_decoder,
        cross_decoder,
    )
    return out[None]


def solution(mesh):
    in_specs = (
        P("layer", None, "width"),
        P("layer", "width", "feat"),
        P("layer", "feat"),
        P(),
        P("layer", "feat", "width"),
        P("feat", "width"),
    )
    out_specs = P("layer", "feat", "width")
    return jax.shard_map(
        on_device, mesh=mesh, in_specs=in_specs, out_specs=out_specs, check_vma=False
    )
```

```python
import functools

import jax
import jax.numpy as jnp
import numpy as np
from jax import lax
from jax.experimental import pallas as pl
from jax.experimental.pallas import tpu as pltpu
from jax.sharding import PartitionSpec as P


BLOCK = 128
MIB = 1 << 20
GRANT = [8 * MIB]
TILE = 4 * BLOCK


def capacities(blocks, listed, shards):
    most = min(blocks, listed)
    fair = -(-listed // shards)
    first = -(-(fair * 4) // 12) * 4
    if most <= first:
        return [(1, -(-most // 2) * 2)]
    once = [(1, first)] + ([(1, first + 4)] if first + 4 < most else [])
    return once + [(-(-most // first), first)]


def target_order(count):
    rows = []
    for i in range(count):
        rows.append(sorted(range(count), key=lambda t: (-abs(t - i), t < i)))
    return rows


def slots_of(active_ref, layer, first, blocks, start, ids):
    slots = ids.shape[0]
    for k in range(slots):
        ids[k] = 0

    def look(k, count):
        block = active_ref[layer, k] - first
        here = (block >= 0) & (block < blocks)

        @pl.when(here & (count >= 0) & (count < slots))
        def _():
            ids[count] = block

        return count + here.astype(jnp.int32)

    return lax.fori_loop(0, active_ref.shape[1], look, -start, unroll=8)


def row_copies(shape, first, place, order, residual, tokens, sems):
    _, width, units, unit = shape
    copies = []
    for k in range(tokens.shape[0] // unit):
        chunk, p, u = (first + k) // (width * units), (first + k) // units % width, (first + k) % units
        row = order[place[1], chunk * units + u] * width + (place[2] ^ p)
        copies.append(
            pltpu.make_async_copy(
                residual.at[pl.ds(pl.multiple_of(row * unit, unit), unit), :],
                tokens.at[k * unit : (k + 1) * unit, :],
                sems.at[k],
            )
        )
    return copies


def rows_kernel(shape, after, place, order, residual, tokens, sems):
    del after
    copies = row_copies(shape, shape[1] * shape[2], place, order, residual, tokens, sems)
    for copy in copies:
        copy.start()
    for copy in copies:
        copy.wait()


def later_rows(after, place, order, residual, width, units, unit):
    early = width * units
    count = residual.shape[0] // unit - early
    smem = pl.BlockSpec(memory_space=pltpu.SMEM)
    anywhere = pl.BlockSpec(memory_space=pl.ANY)
    return pl.pallas_call(
        functools.partial(rows_kernel, (0, width, units, unit)),
        out_shape=jax.ShapeDtypeStruct((count * unit, residual.shape[1]), jnp.bfloat16),
        in_specs=[anywhere, smem, smem, anywhere],
        out_specs=pl.BlockSpec(memory_space=pltpu.VMEM),
        scratch_shapes=[pltpu.SemaphoreType.DMA((count,))],
        compiler_params=pltpu.CompilerParams(vmem_limit_bytes=GRANT[-1]),
        cost_estimate=pl.CostEstimate(
            flops=0, bytes_accessed=2 * count * unit * residual.shape[1], transcendentals=0
        ),
        name="rows",
    )(after, place, order, residual)


def load_kernel(shape, active, place, order, residual, encoder, thresholds, weight, tokens, limit, *refs):
    blocks, width, units, unit = shape
    outs, (ids, sems, more) = refs[:width], refs[width:]
    slots = ids.shape[0]
    tile = 2 * BLOCK
    size = units * unit

    def block_copy(k, block):
        return pltpu.make_async_copy(
            encoder.at[0, :, pl.ds(pl.multiple_of(block * BLOCK, BLOCK), BLOCK)],
            weight.at[:, pl.ds(pl.multiple_of(k * BLOCK, BLOCK), BLOCK)],
            sems.at[k],
        )

    copies = row_copies(shape, 0, place, order, residual, tokens, more)
    for copy in copies:
        copy.start()
    count = slots_of(active, place[0], place[1] * blocks, blocks, place[3], ids)
    for k in range(slots):
        block_copy(k, ids[k]).start()
    for k in range(slots):
        row = thresholds[pl.ds(ids[k], 1), :]
        limit[:, k * BLOCK : (k + 1) * BLOCK] = jnp.where(k < count, row, jnp.inf)
    for copy in copies:
        copy.wait()

    @pl.loop(0, slots // 2)
    def _(n):
        block_copy(2 * n, 0).wait()
        block_copy(2 * n + 1, 0).wait()
        at = pl.ds(pl.multiple_of(n * tile, tile), tile)
        total = jnp.dot(
            tokens[: width * size, :], weight[:, at], preferred_element_type=jnp.float32
        )
        for p, out in enumerate(outs):
            out[:, at] = total[p * size : (p + 1) * size, :].astype(out.dtype)


def load(active, place, order, residual, encoder, thresholds, slots, width, units, unit):
    depth = residual.shape[1]
    feats = slots * BLOCK
    blocks = encoder.shape[2] // BLOCK
    smem = pl.BlockSpec(memory_space=pltpu.SMEM)
    anywhere = pl.BlockSpec(memory_space=pl.ANY)
    vmem = pl.BlockSpec(memory_space=pltpu.VMEM)
    return pl.pallas_call(
        functools.partial(load_kernel, (blocks, width, units, unit)),
        out_shape=[
            jax.ShapeDtypeStruct((depth, feats), jnp.bfloat16),
            jax.ShapeDtypeStruct((width * units * unit, depth), jnp.bfloat16),
            jax.ShapeDtypeStruct((1, feats), jnp.float32),
        ]
        + [
            jax.ShapeDtypeStruct((units * unit, feats), jnp.float32 if p == 0 else jnp.bfloat16)
            for p in range(width)
        ],
        in_specs=[smem, smem, smem, anywhere, anywhere, vmem],
        out_specs=[vmem] * (3 + width),
        scratch_shapes=[
            pltpu.SMEM((slots,), jnp.int32),
            pltpu.SemaphoreType.DMA((slots,)),
            pltpu.SemaphoreType.DMA((width * units,)),
        ],
        compiler_params=pltpu.CompilerParams(vmem_limit_bytes=GRANT[-1]),
        cost_estimate=pl.CostEstimate(
            flops=0, bytes_accessed=2 * depth * (feats + width * units * unit), transcendentals=0
        ),
        name="load",
    )(active, place, order, residual, encoder, thresholds)


def fetch_kernel(blocks, active, place, after, own_w, source_w, own_out, source_out, own_ids, source_ids, sems):
    del after
    first = place[1] * blocks
    slots = own_ids.shape[0]
    slots_of(active, place[0], first, blocks, place[3], own_ids)
    slots_of(active, 0, first, blocks, place[3], source_ids)
    copies = []
    for k in range(slots):
        there = slice(k * BLOCK, (k + 1) * BLOCK)
        source = own_w.at[0, pl.ds(pl.multiple_of(own_ids[k] * BLOCK, BLOCK), BLOCK), :]
        copies.append(pltpu.make_async_copy(source, own_out.at[there, :], sems.at[0, k]))
        source = source_w.at[pl.ds(pl.multiple_of(source_ids[k] * BLOCK, BLOCK), BLOCK), :]
        copies.append(pltpu.make_async_copy(source, source_out.at[there, :], sems.at[1, k]))
    for copy in copies:
        copy.start()
    for copy in copies:
        copy.wait()


def fetch(active, place, after, self_decoder, cross_decoder, slots):
    width = cross_decoder.shape[1]
    blocks = cross_decoder.shape[0] // BLOCK
    smem = pl.BlockSpec(memory_space=pltpu.SMEM)
    anywhere = pl.BlockSpec(memory_space=pl.ANY)
    vmem = pl.BlockSpec(memory_space=pltpu.VMEM)
    return pl.pallas_call(
        functools.partial(fetch_kernel, blocks),
        out_shape=[jax.ShapeDtypeStruct((slots * BLOCK, width), jnp.bfloat16)] * 2,
        in_specs=[smem, smem, anywhere, anywhere, anywhere],
        out_specs=[vmem, vmem],
        scratch_shapes=[
            pltpu.SMEM((slots,), jnp.int32),
            pltpu.SMEM((slots,), jnp.int32),
            pltpu.SemaphoreType.DMA((2, slots)),
        ],
        compiler_params=pltpu.CompilerParams(vmem_limit_bytes=GRANT[-1]),
        cost_estimate=pl.CostEstimate(
            flops=0, bytes_accessed=4 * slots * BLOCK * width, transcendentals=0
        ),
        name="fetch",
    )(active, place, after, self_decoder, cross_decoder)


def encode_kernel(first, after, tokens, weight, *outs):
    del after
    size = outs[0].shape[0]
    count = size * len(outs)
    tile = 2 * BLOCK
    lhs = tokens[first : first + count, :]

    @pl.loop(0, weight.shape[1] // tile)
    def _(n):
        at = pl.ds(pl.multiple_of(n * tile, tile), tile)
        total = jnp.dot(lhs, weight[:, at], preferred_element_type=jnp.float32)
        for p, out in enumerate(outs):
            out[:, at] = total[p * size : (p + 1) * size, :].astype(out.dtype)


def encode(tokens, weight, chunk, chunks, width, after):
    size = tokens.shape[0] // (chunks * width)
    depth, feats = weight.shape
    vmem = pl.BlockSpec(memory_space=pltpu.VMEM)
    return pl.pallas_call(
        functools.partial(encode_kernel, chunk * width * size),
        out_shape=[
            jax.ShapeDtypeStruct((size, feats), jnp.float32 if p == 0 else jnp.bfloat16)
            for p in range(width)
        ],
        in_specs=[pl.BlockSpec(memory_space=pl.ANY), vmem, vmem],
        out_specs=[vmem] * width,
        compiler_params=pltpu.CompilerParams(vmem_limit_bytes=GRANT[-1]),
        cost_estimate=pl.CostEstimate(
            flops=2 * width * size * depth * feats, bytes_accessed=0, transcendentals=0
        ),
        name="encode",
    )(after, tokens, weight)


def combine_kernel(own, limit, *refs):
    out = refs[-1]
    tile = 2 * BLOCK

    @pl.loop(0, out.shape[1] // tile)
    def _(n):
        at = pl.ds(pl.multiple_of(n * tile, tile), tile)
        total = own[:, at]
        for term in refs[:-1]:
            total = total + term[:, at].astype(jnp.float32)
        out[:, at] = jnp.maximum(total - limit[:, at], 0.0).astype(out.dtype)


def combine(own, limit, arrived):
    vmem = pl.BlockSpec(memory_space=pltpu.VMEM)
    return pl.pallas_call(
        combine_kernel,
        out_shape=jax.ShapeDtypeStruct(own.shape, jnp.bfloat16),
        in_specs=[vmem] * (2 + len(arrived)),
        out_specs=vmem,
        compiler_params=pltpu.CompilerParams(vmem_limit_bytes=GRANT[-1]),
        cost_estimate=pl.CostEstimate(flops=0, bytes_accessed=own.size * 4, transcendentals=0),
        name="combine",
    )(own, limit, *arrived)


def pack_kernel(*refs):
    out = refs[-1]
    size = refs[0].shape[0]
    for p, piece in enumerate(refs[:-1]):
        out[p * size : (p + 1) * size, :] = piece[...]


def pack(pieces):
    vmem = pl.BlockSpec(memory_space=pltpu.VMEM)
    size, feats = pieces[0].shape
    return pl.pallas_call(
        pack_kernel,
        out_shape=jax.ShapeDtypeStruct((size * len(pieces), feats), jnp.bfloat16),
        in_specs=[vmem] * len(pieces),
        out_specs=vmem,
        compiler_params=pltpu.CompilerParams(vmem_limit_bytes=GRANT[-1]),
        cost_estimate=pl.CostEstimate(flops=0, bytes_accessed=0, transcendentals=0),
        name="pack",
    )(*pieces)


def decode_kernel(codes, weight, out):
    @pl.loop(0, out.shape[1] // TILE)
    def _(n):
        at = pl.ds(pl.multiple_of(n * TILE, TILE), TILE)
        out[:, at] = jnp.dot(codes[...], weight[:, at], preferred_element_type=jnp.float32)


def decode_more_kernel(codes, weight, base, out, *rounded):
    @pl.loop(0, out.shape[1] // TILE)
    def _(n):
        at = pl.ds(pl.multiple_of(n * TILE, TILE), TILE)
        total = base[:, at] + jnp.dot(
            codes[...], weight[:, at], preferred_element_type=jnp.float32
        )
        out[:, at] = total
        for ref in rounded:
            ref[:, at] = total.astype(ref.dtype)


def decode(codes, weight, base=None, both=True):
    vmem = pl.BlockSpec(memory_space=pltpu.VMEM)
    tokens, feats = codes.shape
    width = weight.shape[1]
    extra = () if base is None else (base,)
    out_shape = [jax.ShapeDtypeStruct((tokens, width), jnp.float32)]
    if base is not None and both:
        out_shape.append(jax.ShapeDtypeStruct((tokens, width), jnp.bfloat16))
    return pl.pallas_call(
        decode_kernel if base is None else decode_more_kernel,
        out_shape=out_shape,
        in_specs=[vmem] * (2 + len(extra)),
        out_specs=[vmem] * len(out_shape),
        compiler_params=pltpu.CompilerParams(vmem_limit_bytes=GRANT[-1]),
        cost_estimate=pl.CostEstimate(
            flops=2 * tokens * feats * width, bytes_accessed=0, transcendentals=0
        ),
        name="decode" if base is None else "decode_more",
    )(codes, weight, *extra)


def relay_kernel(owners, place, *refs):
    came, values, outs = refs[:2], refs[2:-2], refs[-2:]
    for term, out, lists in zip(came, outs, owners, strict=True):
        for devices, value in zip(lists, values, strict=True):
            if not devices:
                continue
            here = functools.reduce(jnp.logical_or, [place[1] == d for d in devices])

            @pl.when(here)
            def _(value=value, term=term, out=out):
                out[...] = (value[...] + term[...].astype(jnp.float32)).astype(out.dtype)


def relay(owners, place, came, values):
    vmem = pl.BlockSpec(memory_space=pltpu.VMEM)
    return pl.pallas_call(
        functools.partial(relay_kernel, owners),
        out_shape=[jax.ShapeDtypeStruct(term.shape, jnp.bfloat16) for term in came],
        in_specs=[pl.BlockSpec(memory_space=pltpu.SMEM)] + [vmem] * (2 + len(values)),
        out_specs=[vmem] * 2,
        compiler_params=pltpu.CompilerParams(vmem_limit_bytes=GRANT[-1]),
        cost_estimate=pl.CostEstimate(
            flops=0, bytes_accessed=8 * came[0].size, transcendentals=0
        ),
        name="relay",
    )(place, *came, *values)


def finish_kernel(place_ref, own, first, second, out):
    del place_ref
    total = own[...] + first[...].astype(jnp.float32) + second[...].astype(jnp.float32)
    out[...] = total.astype(out.dtype)


def finish(place, own, first, second, count):
    tokens, width = own.shape
    spec = pl.BlockSpec((tokens // count, width), lambda p, r: (p, 0))
    return pl.pallas_call(
        finish_kernel,
        out_shape=pltpu.HBM((tokens, width), jnp.bfloat16),
        grid_spec=pltpu.PrefetchScalarGridSpec(
            num_scalar_prefetch=1,
            grid=(count,),
            in_specs=[spec] * 3,
            out_specs=pl.BlockSpec((tokens // count, width), lambda p, r: (r[2] ^ p, 0)),
        ),
        compiler_params=pltpu.CompilerParams(vmem_limit_bytes=8 * MIB),
        name="finish",
    )(place, own, first, second)


def run(passes, slots, residual, encoder, thresholds, active, self_decoder, cross_decoder):
    layer_index = lax.axis_index("layer")
    feat_index = lax.axis_index("feat")
    width_index = lax.axis_index("width")
    feat_count = lax.axis_size("feat")
    width_count = lax.axis_size("width")
    tokens = residual.shape[0]
    chunks = min(4, feat_count)
    units = feat_count // chunks
    block = tokens // feat_count
    unit = block // width_count

    order = target_order(feat_count)
    table = jnp.asarray(np.array(order, np.int32))

    def setup(start):
        spot = [jnp.asarray(n, jnp.int32) for n in (layer_index, feat_index, width_index, start)]
        place = jnp.stack(spot)
        loaded = load(
            active, place, table, residual, encoder, thresholds, slots, width_count, units, unit
        )
        weights = fetch(active, place, loaded[4], self_decoder, cross_decoder, slots)
        rest = later_rows(loaded[4], place, table, residual, width_count, units, unit)
        return place, loaded, rest, weights

    def swap(value, p):
        return lax.ppermute(value, "width", [(w, w ^ p) for w in range(width_count)])

    def spread(values):
        moved = []
        for p, value in enumerate(values, 1):
            moved.append(swap(value, p))
        return moved

    def chunk_of(c, limit, own, others, weights, base=None):
        own_w, source_w = weights
        arrived = spread(others)
        share = combine(own, limit, arrived)
        pieces = [share] + spread([share] * (width_count - 1))
        codes = pack(pieces)
        source = lax.ppermute(codes, "layer", [(0, 1)])
        (base,) = decode(codes, own_w, base, False)
        return decode(source, source_w, base, c == 0)

    results = []
    if passes > 1:
        part = tokens // chunks

        def one_pass(g, kept):
            place, (weight, front, limit, *_), rest, weights = setup(g * slots)
            ordered = jnp.concatenate([front, rest], axis=0)

            def one(c, kept):
                some = lax.dynamic_slice_in_dim(ordered, c * part, part)
                own, *others = encode(some, weight, 0, 1, width_count, limit)
                before = lax.dynamic_slice_in_dim(kept, c * part, part)
                result, _ = chunk_of(0, limit, own, others, weights, before)
                return lax.dynamic_update_slice_in_dim(kept, result, c * part, 0)

            return lax.fori_loop(0, chunks, one, kept)

        kept = jnp.zeros((tokens, cross_decoder.shape[1]), jnp.float32)
        kept = lax.fori_loop(0, passes, one_pass, kept)
        place = jnp.stack([layer_index, feat_index, width_index]).astype(jnp.int32)
        results = [(result, result.astype(jnp.bfloat16)) for result in jnp.split(kept, chunks)]
    else:
        place, (weight, _, limit, own, *others), rest, weights = setup(0)
        for c in range(chunks):
            if c > 0:
                own, *others = encode(rest, weight, c - 1, chunks - 1, width_count, limit)
            results.append(chunk_of(c, limit, own, others, weights))
    decoded = []
    for parts in results:
        for u in range(units):
            if units == 1:
                decoded.append(parts)
                continue
            cut = [part.reshape(width_count, units, unit, -1)[:, u] for part in parts]
            decoded.append([part.reshape(block, -1) for part in cut])

    def next_sums(ways, came):
        if came is None:
            return [decoded[min(way.values())][1] for way in ways]
        used = sorted({position for way in ways for position in way.values()})
        owners = tuple(
            tuple(tuple(d for d, k in way.items() if k == position) for position in used)
            for way in ways
        )
        return relay(owners, place, came, [decoded[k][0] for k in used])

    came = None
    for step in range(1, feat_count):
        up = {i: order[i].index(feat_count - step + i) for i in range(step)}
        down = {
            i: order[i].index(step - feat_count + i)
            for i in range(feat_count - step, feat_count)
        }
        upward, downward = next_sums((up, down), came)
        from_left = lax.ppermute(upward, "feat", [(i, i + 1) for i in sorted(up)])
        from_right = lax.ppermute(downward, "feat", [(i, i - 1) for i in sorted(down)])
        came = (from_left, from_right)
    return finish(place, decoded[-1][0], from_left, from_right, width_count)


def layered(passes, slots, *args):
    if passes == 1:
        return run(passes, slots, *args)
    GRANT.append(40 * MIB)
    try:
        return run(passes, slots, *args)
    finally:
        GRANT.pop()


def on_device(residual, encoder, thresholds, active, self_decoder, cross_decoder):
    feat_count = lax.axis_size("feat")
    blocks = encoder.shape[2] // BLOCK
    low = blocks * jnp.arange(feat_count, dtype=jnp.int32)[None, :, None]
    inside = (active[:, None, :] >= low) & (active[:, None, :] < low + blocks)
    counts = jnp.sum(inside.astype(jnp.int32), axis=2)
    most = jnp.max(counts)
    sizes = capacities(blocks, active.shape[1], feat_count)
    branch = sum((most > s).astype(jnp.int32) for _, s in sizes[:-1]) if len(sizes) > 1 else 0
    out = lax.switch(
        branch,
        [functools.partial(layered, *size) for size in sizes],
        residual[0],
        encoder,
        thresholds[0].reshape(-1, BLOCK),
        active,
        self_decoder,
        cross_decoder,
    )
    return out[None]


def solution(mesh):
    in_specs = (
        P("layer", None, "width"),
        P("layer", "width", "feat"),
        P("layer", "feat"),
        P(),
        P("layer", "feat", "width"),
        P("feat", "width"),
    )
    out_specs = P("layer", "feat", "width")
    return jax.shard_map(
        on_device, mesh=mesh, in_specs=in_specs, out_specs=out_specs, check_vma=False
    )
```
